512 devices in a mesh: mom: 32 (over z, core), hist: 16 (over y, x).
Axes of the slice: x: 4, y: 4, z: 16, core: 2. Of those that a mesh axis runs over, the one named last changes fastest.
Arguments:
- green_hist: float32 [2, 2, 2, 4096, 4096], P(None, None, None, 'mom', 'hist'), may hold values from 0.5 to 1.5
- sigma_row: float32 [2, 2, 2, 4096], P(None, None, None, 'hist'), may hold values from -6 to 6
- coupling_row: float32 [2, 2, 2, 4096], P(None, None, None, 'hist'), may hold values from -3 to 3
- prop_prev: float32 [2, 2, 2, 4096], P(None, None, None, 'mom'), may hold values from 0.5 to 1.5
- init_state: float32 [4], replicated, may hold values from 0.5 to 1.5
- state_rates: float32 [4], replicated, may hold values from 0.05 to 2
- source_row: float32 [4, 4096], P(None, 'hist'), may hold values from -6 to 6
- mom_ids: int32 [4096], P('mom'), may hold values from 0 to 4095, each once
- t_step: int32 [1], replicated, may hold values from 0 to 2999
- block_len: int32 [16], replicated, may hold values from 1 to 256, 2560 in all
Outputs:
- prop_new: float32 [2, 2, 2, 4096], P(None, None, None, 'mom')
- pp_row: float32 [4, 4096], P(None, 'hist')
- hyb_row: float32 [2, 2, 2, 4096], P(None, None, None, 'hist')
The draws below stay inside these ranges and needn't reach their ends.
Inputs may be any that keep to these rules, and one draw needn't show every extreme that they name: `mom_ids`: each momentum point 0 .. 4095 appears once. `block_len`: the entries sum to 2560; the largest is 256.
All inputs are finite; a program needn't handle non-finite values.
Results may differ from the reference program's by a relative error of at most 0.00035.
Values sent between devices are 32-bit elements; how exact they have to be, the bound alone decides.
A program may use at most 64 MiB of HBM per device.

```python
import math
import jax
import jax.numpy as jnp
import numpy as np
from jax import lax

NO = 2
NP = 4
LK = 64
HB = 256
K = 4096
NH = 4096
T_NOW = 2560
N_HIST = 16


def level_of(own_key, shape, pieces, least, largest):
    factor_of, own = 1.0, jax.random.fold_in(own_key, 6)
    for axis_at, shards_of in pieces:
        heights = jnp.exp(jax.random.uniform(jax.random.fold_in(own, axis_at), (shards_of,), jnp.float32, least / len(pieces), largest / len(pieces)))
        factor_of = factor_of * jnp.repeat(heights, shape[axis_at] // shards_of).reshape([-1 if axis == axis_at else 1 for axis in range(len(shape))])
    return factor_of


def split_up(amount, total, most, skew):
    loads = [(1 << 20) // math.isqrt(grade ** skew) + 1 for grade in range(2, amount + 1)]
    surplus, counts = total - most - (amount - 1), [1] * (amount - 1)
    while surplus > 0:
        candidates = [i for i in range(amount - 1) if counts[i] < most]
        pool, remaining = sum([loads[i] for i in candidates]), surplus
        for i in candidates:
            extra = min(most - counts[i], max(1, remaining * loads[i] // pool), surplus)
            counts[i] = counts[i] + extra
            surplus = surplus - extra
    return np.array([most] + counts)


def ragged(rng, count, total, most, slope):
    if count == 2:
        one = jax.random.randint(rng, (), max(1, total - most), min(most, total - 1) + 1)
        return jnp.stack([one, total - one])
    tallies = jnp.asarray(split_up(count, total, most, slope), jnp.int32)
    pairs = (count - 1) // 2
    donor, taker = tallies[1:1 + 2 * pairs:2], tallies[2:2 + 2 * pairs:2]
    margin = jnp.minimum(donor - 1, most - taker)
    passed = jax.random.randint(jax.random.fold_in(rng, 1), (pairs,), 0, 1 << 20) % (margin + 1)
    tallies = tallies.at[1:1 + 2 * pairs:2].set(donor - passed).at[2:2 + 2 * pairs:2].set(taker + passed)
    return tallies[jax.random.permutation(jax.random.fold_in(rng, 2), count)]


def scatter_about(key, shape, scale, most, cuts=(), held_as=jnp.bfloat16):
    array = jax.random.normal(key, shape, jnp.float32) * scale
    if len(cuts) > 0:
        array = level_of(key, shape, cuts, -0.22, 0.18) * array
    return jnp.clip(array, min=-most, max=most).astype(held_as)


def setup_inputs(seed: int = 0) -> dict:
    key_of = jax.random.split(jax.random.key(seed), 11)
    return {
        "green_hist": jnp.clip(0.5 + 1.0 * jax.random.uniform(key_of[0], (2, NO, NO, K, NH), jnp.float32) ** level_of(key_of[0], (2, NO, NO, K, NH), ((3, 32), (4, 16)), -0.2, 0.2), 0.5, 1.5),
        "sigma_row": scatter_about(key_of[1], (2, NO, NO, NH), 1.0, 6.0, ((3, 16),), jnp.float32),
        "coupling_row": scatter_about(key_of[2], (2, NO, NO, NH), 0.5, 3.0, ((3, 16),), jnp.float32),
        "prop_prev": jnp.clip(0.5 + 1.0 * jax.random.uniform(key_of[3], (2, NO, NO, K), jnp.float32) ** level_of(key_of[3], (2, NO, NO, K), ((3, 32),), -0.2, 0.2), 0.5, 1.5),
        "init_state": jnp.clip(jax.random.uniform(key_of[4], (NP,), jnp.float32, 0.5, 1.5), 0.5, 1.5),
        "state_rates": jnp.clip(jnp.exp(jax.random.uniform(key_of[5], (NP,), jnp.float32, math.log(0.05), math.log(2.0))), 0.05, 2.0),
        "source_row": scatter_about(key_of[6], (NP, NH), 1.0, 6.0, ((1, 16),), jnp.float32),
        "mom_ids": jax.random.permutation(key_of[7], K).astype(jnp.int32),
        "t_step": jax.random.randint(key_of[8], (1,), 0, 3000).astype(jnp.int32),
        "block_len": ragged(key_of[9], N_HIST, T_NOW, HB, 2).astype(jnp.int32),
    }


TIME_STEP = 0.005
HOPPING_TIME = 0.5
FIELD_STEP = 0.0025

def parity_sign(value):
    sign_value = 1
    for position in range(4):
        if value >> position & 1:
            sign_value = -sign_value
    return sign_value

def fock_table():
    table = np.zeros((2, 2, 4, 4), np.float32)
    for state_in in range(4):
        for orb_b in range(2):
            if state_in >> orb_b & 1:
                sign_b = parity_sign(state_in & (1 << orb_b) - 1)
                middle = state_in ^ 1 << orb_b
                for orb_a in range(2):
                    if not middle >> orb_a & 1:
                        sign_a = parity_sign(middle & (1 << orb_a) - 1)
                        state_out = middle | 1 << orb_a
                        table[orb_a, orb_b, state_out, state_in] += sign_a * sign_b
    return jnp.asarray(table, jnp.float32)

def complex_product(left, right):
    hp = lax.Precision.HIGHEST
    real_part = jnp.einsum('ab...,bc...->ac...', left[0], right[0], precision=hp) - jnp.einsum('ab...,bc...->ac...', left[1], right[1], precision=hp)
    imag_part = jnp.einsum('ab...,bc...->ac...', left[0], right[1], precision=hp) + jnp.einsum('ab...,bc...->ac...', left[1], right[0], precision=hp)
    return jnp.stack([real_part, imag_part])

def memory_sum(weighted, history):
    hp = lax.Precision.HIGHEST
    real_part = jnp.einsum('abs,bcks->ack', weighted[0], history[0], precision=hp) - jnp.einsum('abs,bcks->ack', weighted[1], history[1], precision=hp)
    imag_part = jnp.einsum('abs,bcks->ack', weighted[0], history[1], precision=hp) + jnp.einsum('abs,bcks->ack', weighted[1], history[0], precision=hp)
    return jnp.stack([real_part, imag_part])

def row_product(current, history):
    hp = lax.Precision.HIGHEST
    real_part = jnp.einsum('ack,bcks->abs', current[0], history[0], precision=hp) + jnp.einsum('ack,bcks->abs', current[1], history[1], precision=hp)
    imag_part = jnp.einsum('ack,bcks->abs', current[1], history[0], precision=hp) - jnp.einsum('ack,bcks->abs', current[0], history[1], precision=hp)
    return jnp.stack([real_part, imag_part])

def momentum_phase(mom_ids, t_step, total):
    field = FIELD_STEP * t_step[0].astype(jnp.float32)
    along_x = 2.0 * math.pi * (mom_ids % LK).astype(jnp.float32) / LK
    along_y = 2.0 * math.pi * (mom_ids // LK).astype(jnp.float32) / (total // LK)
    energy = -2.0 * (jnp.cos(along_x - field) + jnp.cos(along_y - field))
    angle = HOPPING_TIME * energy
    return (jnp.cos(angle), jnp.sin(angle))

def advance(previous, memory, cosine, sine):
    summed = previous + memory
    real_part = cosine * summed[0] + sine * summed[1]
    imag_part = cosine * summed[1] - sine * summed[0]
    return jnp.stack([real_part, imag_part])

def transitions(delta, live_mask, state_rates, source):
    table = fock_table()
    lam = jnp.einsum('abs,abnm->snm', delta[0], table, precision=lax.Precision.HIGHEST)
    retain = jnp.diag(jnp.exp(-state_rates / NH))
    mats = jnp.where(live_mask[:, None, None], retain[None] - TIME_STEP * lam, jnp.eye(NP, dtype=jnp.float32)[None])
    vecs = jnp.where(live_mask[:, None], TIME_STEP * source.T, jnp.float32(0.0))
    return (mats, vecs)

def reference(green_hist, sigma_row, coupling_row, prop_prev, init_state, state_rates, source_row, mom_ids, t_step, block_len):
    slots = jnp.arange(NH, dtype=jnp.int32)
    live_mask = slots % HB < block_len[slots // HB]
    weight = jnp.where(live_mask, jnp.float32(TIME_STEP), jnp.float32(0.0))
    memory = memory_sum(sigma_row * weight, green_hist)
    cosine, sine = momentum_phase(mom_ids, t_step, K)
    prop_new = advance(prop_prev, memory, cosine, sine)
    local_row = row_product(prop_new, green_hist) / K
    local_row = jnp.where(live_mask, local_row, jnp.float32(0.0))
    delta = complex_product(local_row, coupling_row)
    mats, vecs = transitions(delta, live_mask, state_rates, source_row)

    def step_fn(state, pair):
        new_state = jnp.dot(pair[0], state, precision=lax.Precision.HIGHEST) + pair[1]
        return (new_state, new_state)
    final_state, states = lax.scan(step_fn, init_state, (mats, vecs))
    pp_row = states.T
    scale = 1.0 / jnp.sqrt(1.0 + jnp.sum(final_state * final_state))
    hyb_row = delta * scale
    return (prop_new, pp_row, hyb_row)
```

```python
import functools
import math

import jax
import jax.numpy as jnp
import numpy as np
from jax import lax
from jax.experimental import pallas as pl
from jax.experimental.pallas import tpu as pltpu
from jax.sharding import PartitionSpec as P

MESH = pl.DeviceIdType.MESH
LK = 64
TIME_STEP = 0.005
HOPPING_TIME = 0.5
FIELD_STEP = 0.0025
NX = 4
TILE = (8, 128)
IDENTITY = (1.0, 1.0, 0.0, 0.0, 1.0, 1.0, 0.0, 0.0, 0.0, 0.0)


def compose(late, early):
    l0, l11, l12, l21, l22, l3, lv0, lv1, lv2, lv3 = late
    e0, e11, e12, e21, e22, e3, ev0, ev1, ev2, ev3 = early
    return (
        l0 * e0,
        l11 * e11 + l12 * e21,
        l11 * e12 + l12 * e22,
        l21 * e11 + l22 * e21,
        l21 * e12 + l22 * e22,
        l3 * e3,
        l0 * ev0 + lv0,
        (l11 * ev1 + l12 * ev2) + lv1,
        (l21 * ev1 + l22 * ev2) + lv2,
        l3 * ev3 + lv3,
    )


def apply_map(parts, state):
    m0, a11, a12, a21, a22, m3, v0, v1, v2, v3 = parts
    s0, s1, s2, s3 = state
    return (
        m0 * s0 + v0,
        (a11 * s1 + a12 * s2) + v1,
        (a21 * s1 + a22 * s2) + v2,
        m3 * s3 + v3,
    )


def split(value):
    high = value.astype(jnp.bfloat16)
    low = (value - high.astype(jnp.float32)).astype(jnp.bfloat16)
    return high, low


def split_rows(value):
    high = value.astype(jnp.bfloat16).astype(jnp.float32)
    return jnp.concatenate([high, value - high], axis=0)


def halves(value):
    return jnp.concatenate([value[:, :128], value[:, 128:]], axis=0)


def far_first(count):
    def hops(step):
        return min(step, count - step)

    return sorted(range(1, count), key=lambda step: -hops(step))


def kernel(
    sizes,
    green,
    sigma,
    coupling,
    prev,
    init,
    rates,
    source,
    ids,
    t_step,
    lengths,
    prop_out,
    pp_out,
    hyb_out,
    g_vm,
    ghi,
    glo,
    sig_vm,
    coup_vm,
    prev_vm,
    src_vm,
    ids_vm,
    init_sm,
    rates_sm,
    t_sm,
    len_sm,
    a_buf,
    zr_buf,
    zi_buf,
    pr_buf,
    pi_buf,
    c_buf,
    c_rows,
    local_sem,
    send_sem,
    recv_sem,
    token_sem,
):
    n_mom, n_hist = sizes
    n_z = n_mom // 2
    n_y = n_hist // NX if n_hist >= NX else 1
    n_x = n_hist // n_y
    total = 128 * n_mom
    slots = 256 * n_hist
    mom, hist = lax.axis_index("mom"), lax.axis_index("hist")
    z, core = mom // 2, mom % 2
    y, x = hist // n_x, hist % n_x

    def hop(count, step):
        return min(step, count - step)

    hist_steps = sorted(
        [(dy, dx) for dy in range(n_y) for dx in range(n_x) if (dy, dx) != (0, 0)],
        key=lambda s: -(hop(n_y, s[0]) + hop(n_x, s[1])),
    )
    z_steps = far_first(n_z)

    def hist_peer(step):
        return (mom, ((y + step[0]) % n_y) * n_x + (x + step[1]) % n_x)

    def z_peer(step):
        return (((z + step) % n_z) * 2 + core, hist)

    partner = (z * 2 + 1 - core, hist)

    barrier = pltpu.get_barrier_semaphore()
    near = [hist_peer(step) for step in hist_steps] + [z_peer(1), z_peer(n_z - 1), partner]
    for peer in near:
        pl.semaphore_signal(barrier, inc=1, device_id=peer, device_id_type=MESH)
    small = [
        (sigma, sig_vm),
        (lengths, len_sm),
        (prev, prev_vm),
        (ids, ids_vm),
        (t_step, t_sm),
        (coupling, coup_vm),
        (source, src_vm),
        (rates, rates_sm),
        (init, init_sm),
    ]
    small_copies = [
        pltpu.make_async_copy(src, dst, local_sem.at[4 + i]) for i, (src, dst) in enumerate(small)
    ]
    green_copies = [
        pltpu.make_async_copy(green.at[r, b], g_vm.at[r, b], local_sem.at[2 * r + b])
        for r in range(2)
        for b in range(2)
    ]
    for copy in small_copies[:2]:
        copy.start()
    for copy in green_copies:
        copy.start()
    for copy in small_copies[2:]:
        copy.start()
    for copy in small_copies[:2]:
        copy.wait()

    length = len_sm[hist]
    lane256 = lax.broadcasted_iota(jnp.int32, (1, 256), 1)
    live256 = lane256 < length
    weight = jnp.where(live256, jnp.float32(TIME_STEP), jnp.float32(0.0))
    pad8 = jnp.zeros((8, 256), jnp.float32)
    left_sides = {}
    for b in range(2):
        re = [sig_vm[0, a, b : b + 1, :] * weight for a in range(2)]
        im = [sig_vm[1, a, b : b + 1, :] * weight for a in range(2)]
        for r, rows in ((0, re + im), (1, [-im[0], -im[1]] + re)):
            stacked = split_rows(jnp.concatenate(rows, axis=0))
            left_sides[r, b] = jnp.concatenate([stacked, pad8], axis=0).astype(jnp.bfloat16)
    acc = jnp.zeros((16, 256), jnp.float32)
    contract_last = (((1,), (1,)), ((), ()))
    for r in range(2):
        for b in range(2):
            green_copies[2 * r + b].wait()
            high, low = split(g_vm[r, b].reshape(256, 256))
            ghi[r, b] = high
            glo[r, b] = low
            for part in (high, low):
                acc += lax.dot_general(
                    left_sides[r, b], part, contract_last, preferred_element_type=jnp.float32
                )
    mem4 = acc[0:4] + acc[4:8]
    a_buf[hist] = halves(mem4)

    pl.semaphore_wait(barrier, len(near))

    def send(buf, slot, which, peer):
        pltpu.make_async_remote_copy(
            src_ref=buf.at[slot],
            dst_ref=buf.at[slot],
            send_sem=send_sem.at[which],
            recv_sem=recv_sem.at[which],
            device_id=peer,
            device_id_type=MESH,
        ).start()

    def arrived(sem, buf, which, count):
        part = buf.at[pl.ds(0, count)]
        pltpu.make_async_copy(part, part, sem.at[which]).wait()

    for step in hist_steps:
        send(a_buf, hist, 0, hist_peer(step))

    reach = 1
    token = 0
    while reach < n_z // 2:
        for peer in (z_peer(reach), z_peer(n_z - reach)):
            pl.semaphore_signal(token_sem.at[token], inc=1, device_id=peer, device_id_type=MESH)
        if 2 * reach < n_z // 2:
            pl.semaphore_wait(token_sem.at[token], 2)
        reach *= 2
        token += 1

    for copy in small_copies[2:]:
        copy.wait()

    row = lax.broadcasted_iota(jnp.int32, TILE, 0)
    lane = lax.broadcasted_iota(jnp.int32, TILE, 1)
    field = jnp.full((1, 128), t_sm[0], jnp.int32).astype(jnp.float32) * FIELD_STEP
    momentum = ids_vm[...].reshape(1, 128)
    along_x = 2.0 * math.pi * (momentum & (LK - 1)).astype(jnp.float32) / LK
    along_y = 2.0 * math.pi * (momentum >> 6).astype(jnp.float32) / (total // LK)
    energy = -2.0 * (jnp.cos(along_x - field) + jnp.cos(along_y - field))
    angle = HOPPING_TIME * energy
    cosine = jnp.broadcast_to(jnp.cos(angle), TILE)
    sine = jnp.broadcast_to(jnp.sin(angle), TILE)
    before = jnp.concatenate(
        [prev_vm[r, a, c : c + 1, :] for c in range(2) for r in range(2) for a in range(2)], axis=0
    )
    is_real = (row & 2) == 0

    live_scale = jnp.where(live256, jnp.float32(1.0 / total), jnp.float32(0.0))
    real_side, imag_side = [], []
    for b in range(2):
        cr = coup_vm[0, b] * live_scale
        ci = coup_vm[1, b] * live_scale
        real_side.append(jnp.concatenate([cr, cr, -ci, -ci], axis=0))
        imag_side.append(jnp.concatenate([ci, ci, cr, cr], axis=0))

    upper = row >= 4
    live = jnp.where(upper, lane + 128, lane) < length
    drives = halves(src_vm[...])
    drive_scale = jnp.where(live, jnp.float32(TIME_STEP), jnp.float32(0.0))

    def bring(value, index):
        return pltpu.roll(value, 8 - index, axis=0) if index else value

    drive = [bring(drives, n) * drive_scale for n in range(4)]
    retain = []
    for n in range(4):
        decay = jnp.exp(-(jnp.full(TILE, rates_sm[n], jnp.float32) / slots))
        retain.append(jnp.where(live, decay, jnp.float32(1.0)))

    arrived(recv_sem, a_buf, 0, n_hist - 1)
    memory = a_buf[0]
    for h in range(1, n_hist):
        memory = memory + a_buf[h]
    summed = before + memory
    swapped = jnp.where(is_real, pltpu.roll(summed, 6, axis=0), -pltpu.roll(summed, 2, axis=0))
    current = cosine * summed + sine * swapped
    for c in range(2):
        for r in range(2):
            for a in range(2):
                at = 4 * c + 2 * r + a
                prop_out[r, a, c : c + 1, :] = current[at : at + 1, :]

    straight = jnp.concatenate([current[0:4], current[4:8]], axis=1)
    turned = jnp.concatenate([straight[2:4], -straight[0:2]], axis=0)
    rows = []
    for side in (straight, turned):
        twice = jnp.concatenate([side[i // 2 : i // 2 + 1] for i in range(8)], axis=0)
        rows.append(split_rows(twice).astype(jnp.bfloat16))
    contract_first = (((1,), (0,)), ((), ()))
    real_sum, imag_sum = None, None
    for b in range(2):
        out = jnp.zeros((16, 256), jnp.float32)
        for r in range(2):
            for part in (ghi, glo):
                out += lax.dot_general(
                    rows[r], part[r, b], contract_first, preferred_element_type=jnp.float32
                )
        both = out[0:8] + out[8:16]
        re, im = both * real_side[b], both * imag_side[b]
        real_sum = re if b == 0 else real_sum + re
        imag_sum = im if b == 0 else imag_sum + im

    def fold(value):
        first, second = value[:, :128], value[:, 128:]
        first = first + pltpu.roll(first, 4, axis=0)
        second = second + pltpu.roll(second, 4, axis=0)
        return jnp.where(upper, second, first)

    zr_buf[z] = fold(real_sum)
    zi_buf[z] = fold(imag_sum)
    if token:
        pl.semaphore_wait(token_sem.at[token - 1], 2)
    for step in z_steps:
        send(zr_buf, z, 1, z_peer(step))
    for step in z_steps:
        send(zi_buf, z, 2, z_peer(step))

    def total_over_z(buf, which):
        arrived(recv_sem, buf, which, n_z - 1)
        value = buf[0]
        for i in range(1, n_z):
            value = value + buf[i]
        return value

    pr_buf[core] = total_over_z(zr_buf, 1)
    send(pr_buf, core, 3, partner)
    arrived(recv_sem, pr_buf, 3, 1)
    delta_re = pr_buf[0] + pr_buf[1]

    d00, d01, d10, d11 = (TIME_STEP * bring(delta_re, i) for i in range(4))
    maps = (
        retain[0],
        retain[1] - d00,
        -d01,
        -d10,
        retain[2] - d11,
        retain[3] - (d00 + d11),
        *drive,
    )
    shift = 1
    while shift < 128:
        inside = lane >= shift
        early = tuple(
            jnp.where(inside, pltpu.roll(part, shift, axis=1), jnp.float32(one))
            for part, one in zip(maps, IDENTITY)
        )
        maps = compose(maps, early)
        shift *= 2
    ends = tuple(jnp.broadcast_to(part[:, 127:128], TILE) for part in maps)
    first_half = tuple(pltpu.roll(part, 4, axis=0) for part in ends)
    block = compose(ends, first_half)
    packed = jnp.zeros(TILE, jnp.float32)
    for i, part in enumerate(block):
        packed = jnp.where(lane == i, part, packed)
    c_buf[hist] = packed[4:5, :]
    for step in hist_steps:
        send(c_buf, hist, 5, hist_peer(step))

    prefix = compose(
        maps,
        tuple(
            jnp.where(upper, part, jnp.float32(one)) for part, one in zip(first_half, IDENTITY)
        ),
    )
    pi_buf[core] = total_over_z(zi_buf, 2)
    send(pi_buf, core, 4, partner)

    arrived(recv_sem, c_buf, 5, n_hist - 1)
    gathered = c_buf[...].reshape(n_hist, 128)
    for i in range(10):
        c_rows[i] = jnp.broadcast_to(gathered[:, i : i + 1], (n_hist, 128))
    state = tuple(jnp.full((1, 128), init_sm[n], jnp.float32) for n in range(4))
    start = state
    for j in range(n_hist):
        state = apply_map(tuple(c_rows[i, j : j + 1, :] for i in range(10)), state)
        if j + 1 < n_hist:
            mine = hist == j + 1
            start = tuple(jnp.where(mine, new, old) for new, old in zip(state, start))
    states = apply_map(prefix, tuple(jnp.broadcast_to(part, TILE) for part in start))
    for n in range(4):
        pp_out[n : n + 1, 0:128] = states[n][0:1]
        pp_out[n : n + 1, 128:256] = states[n][4:5]
    norm = state[0] * state[0] + state[1] * state[1] + state[2] * state[2] + state[3] * state[3]
    scale = jnp.broadcast_to(1.0 / jnp.sqrt(1.0 + norm), TILE)
    arrived(recv_sem, pi_buf, 4, 1)
    delta_im = pi_buf[0] + pi_buf[1]
    for r, delta in ((0, delta_re), (1, delta_im)):
        scaled = delta * scale
        for a in range(2):
            for half in range(2):
                hyb_out[r, a, :, half * 128 : half * 128 + 128] = scaled[
                    half * 4 + 2 * a : half * 4 + 2 * a + 2
                ]

    for buf, which, count in (
        (a_buf, 0, n_hist - 1),
        (zr_buf, 1, n_z - 1),
        (zi_buf, 2, n_z - 1),
        (pr_buf, 3, 1),
        (pi_buf, 4, 1),
        (c_buf, 5, n_hist - 1),
    ):
        arrived(send_sem, buf, which, count)


def on_device(sizes, *args):
    f32 = jnp.float32
    n_mom, n_hist = sizes
    n_z = n_mom // 2
    hbm = pl.BlockSpec(memory_space=pl.ANY)
    vmem = pl.BlockSpec(memory_space=pltpu.VMEM)
    return pl.pallas_call(
        functools.partial(kernel, sizes),
        out_shape=(
            jax.ShapeDtypeStruct((2, 2, 2, 128), f32),
            jax.ShapeDtypeStruct((4, 256), f32),
            jax.ShapeDtypeStruct((2, 2, 2, 256), f32),
        ),
        in_specs=[hbm] * 10,
        out_specs=(vmem, vmem, vmem),
        scratch_shapes=[
            pltpu.VMEM((2, 2, 2, 128, 256), f32),
            pltpu.VMEM((2, 2, 256, 256), jnp.bfloat16),
            pltpu.VMEM((2, 2, 256, 256), jnp.bfloat16),
            pltpu.VMEM((2, 2, 2, 256), f32),
            pltpu.VMEM((2, 2, 2, 256), f32),
            pltpu.VMEM((2, 2, 2, 128), f32),
            pltpu.VMEM((4, 256), f32),
            pltpu.VMEM((128,), jnp.int32),
            pltpu.SMEM((4,), f32),
            pltpu.SMEM((4,), f32),
            pltpu.SMEM((1,), jnp.int32),
            pltpu.SMEM((n_hist,), jnp.int32),
            pltpu.VMEM((n_hist, 8, 128), f32),
            pltpu.VMEM((n_z, 8, 128), f32),
            pltpu.VMEM((n_z, 8, 128), f32),
            pltpu.VMEM((2, 8, 128), f32),
            pltpu.VMEM((2, 8, 128), f32),
            pltpu.VMEM((n_hist, 1, 128), f32),
            pltpu.VMEM((10, n_hist, 128), f32),
            pltpu.SemaphoreType.DMA((13,)),
            pltpu.SemaphoreType.DMA((6,)),
            pltpu.SemaphoreType.DMA((6,)),
            pltpu.SemaphoreType.REGULAR((4,)),
        ],
        compiler_params=pltpu.CompilerParams(collective_id=0, has_side_effects=True),
        name="dmft_step",
    )(*args)


def solution(mesh):
    sizes = (mesh.shape["mom"], mesh.shape["hist"])
    placed = (
        P(None, None, None, "mom", "hist"),
        P(None, None, None, "hist"),
        P(None, None, None, "hist"),
        P(None, None, None, "mom"),
        P(),
        P(),
        P(None, "hist"),
        P("mom"),
        P(),
        P(),
    )
    return jax.shard_map(
        functools.partial(on_device, sizes),
        mesh=mesh,
        in_specs=placed,
        out_specs=(P(None, None, None, "mom"), P(None, "hist"), P(None, None, None, "hist")),
        check_vma=False,
    )
```

```python
import functools
import math

import jax
import jax.numpy as jnp
import numpy as np
from jax import lax
from jax.experimental import pallas as pl
from jax.experimental.pallas import tpu as pltpu
from jax.sharding import PartitionSpec as P

MESH = pl.DeviceIdType.MESH
LK = 64
TIME_STEP = 0.005
HOPPING_TIME = 0.5
FIELD_STEP = 0.0025
NX = 4
TILE = (8, 128)
IDENTITY = (1.0, 1.0, 0.0, 0.0, 1.0, 1.0, 0.0, 0.0, 0.0, 0.0)


def compose(late, early):
    l0, l11, l12, l21, l22, l3, lv0, lv1, lv2, lv3 = late
    e0, e11, e12, e21, e22, e3, ev0, ev1, ev2, ev3 = early
    return (
        l0 * e0,
        l11 * e11 + l12 * e21,
        l11 * e12 + l12 * e22,
        l21 * e11 + l22 * e21,
        l21 * e12 + l22 * e22,
        l3 * e3,
        l0 * ev0 + lv0,
        (l11 * ev1 + l12 * ev2) + lv1,
        (l21 * ev1 + l22 * ev2) + lv2,
        l3 * ev3 + lv3,
    )


def apply_map(parts, state):
    m0, a11, a12, a21, a22, m3, v0, v1, v2, v3 = parts
    s0, s1, s2, s3 = state
    return (
        m0 * s0 + v0,
        (a11 * s1 + a12 * s2) + v1,
        (a21 * s1 + a22 * s2) + v2,
        m3 * s3 + v3,
    )


def split(value):
    high = value.astype(jnp.bfloat16)
    low = (value - high.astype(jnp.float32)).astype(jnp.bfloat16)
    return high, low


def split_rows(value):
    high = value.astype(jnp.bfloat16).astype(jnp.float32)
    return jnp.concatenate([high, value - high], axis=0)


def halves(value):
    return jnp.concatenate([value[:, :128], value[:, 128:]], axis=0)


def far_first(count):
    def hops(step):
        return min(step, count - step)

    return sorted(range(1, count), key=lambda step: -hops(step))


def kernel(
    sizes,
    green,
    sigma,
    coupling,
    prev,
    init,
    rates,
    source,
    ids,
    t_step,
    lengths,
    prop_out,
    pp_out,
    hyb_out,
    g_vm,
    ghi,
    glo,
    sig_vm,
    coup_vm,
    prev_vm,
    src_vm,
    ids_vm,
    init_sm,
    rates_sm,
    t_sm,
    len_sm,
    a_buf,
    zr_buf,
    zi_buf,
    pr_buf,
    pi_buf,
    c_buf,
    c_rows,
    local_sem,
    send_sem,
    recv_sem,
    token_sem,
):
    n_mom, n_hist = sizes
    n_z = n_mom // 2
    n_y = n_hist // NX if n_hist >= NX else 1
    n_x = n_hist // n_y
    total = 128 * n_mom
    slots = 256 * n_hist
    mom, hist = lax.axis_index("mom"), lax.axis_index("hist")
    z, core = mom // 2, mom % 2
    y, x = hist // n_x, hist % n_x

    def hop(count, step):
        return min(step, count - step)

    hist_steps = sorted(
        [(dy, dx) for dy in range(n_y) for dx in range(n_x) if (dy, dx) != (0, 0)],
        key=lambda s: -(hop(n_y, s[0]) + hop(n_x, s[1])),
    )
    z_steps = far_first(n_z)

    def hist_peer(step):
        return (mom, ((y + step[0]) % n_y) * n_x + (x + step[1]) % n_x)

    def z_peer(step):
        return (((z + step) % n_z) * 2 + core, hist)

    partner = (z * 2 + 1 - core, hist)

    barrier = pltpu.get_barrier_semaphore()
    reach = n_z // 4
    near_z = sorted({step % n_z for r in range(1, reach + 1) for step in (r, -r)})
    near = [hist_peer(step) for step in hist_steps] + [z_peer(step) for step in near_z]
    near.append(partner)
    far_z = (z_peer(reach), z_peer(n_z - reach))
    for peer in near:
        pl.semaphore_signal(barrier, inc=1, device_id=peer, device_id_type=MESH)
    small = [
        (sigma, sig_vm),
        (lengths, len_sm),
        (prev, prev_vm),
        (ids, ids_vm),
        (t_step, t_sm),
        (coupling, coup_vm),
        (source, src_vm),
        (rates, rates_sm),
        (init, init_sm),
    ]
    small_copies = [
        pltpu.make_async_copy(src, dst, local_sem.at[4 + i]) for i, (src, dst) in enumerate(small)
    ]
    green_copies = [
        pltpu.make_async_copy(green.at[r, b], g_vm.at[r, b], local_sem.at[2 * r + b])
        for r in range(2)
        for b in range(2)
    ]
    for copy in small_copies[:2]:
        copy.start()
    for copy in green_copies:
        copy.start()
    for copy in small_copies[2:]:
        copy.start()

    for copy in small_copies[:2]:
        copy.wait()

    length = len_sm[hist]
    lane256 = lax.broadcasted_iota(jnp.int32, (1, 256), 1)
    live256 = lane256 < length
    weight = jnp.where(live256, jnp.float32(TIME_STEP), jnp.float32(0.0))
    pad8 = jnp.zeros((8, 256), jnp.float32)
    left_sides = {}
    for b in range(2):
        re = [sig_vm[0, a, b : b + 1, :] * weight for a in range(2)]
        im = [sig_vm[1, a, b : b + 1, :] * weight for a in range(2)]
        for r, rows in ((0, re + im), (1, [-im[0], -im[1]] + re)):
            stacked = split_rows(jnp.concatenate(rows, axis=0))
            left_sides[r, b] = jnp.concatenate([stacked, pad8], axis=0).astype(jnp.bfloat16)
    acc = jnp.zeros((16, 256), jnp.float32)
    contract_last = (((1,), (1,)), ((), ()))
    for r in range(2):
        for b in range(2):
            green_copies[2 * r + b].wait()
            high, low = split(g_vm[r, b].reshape(256, 256))
            ghi[r, b] = high
            glo[r, b] = low
            for part in (high, low):
                acc += lax.dot_general(
                    left_sides[r, b], part, contract_last, preferred_element_type=jnp.float32
                )
    mem4 = acc[0:4] + acc[4:8]
    a_buf[hist] = halves(mem4)

    pl.semaphore_wait(barrier, len(near))
    for peer in far_z:
        pl.semaphore_signal(token_sem.at[0], inc=1, device_id=peer, device_id_type=MESH)

    def send(buf, slot, which, peer):
        pltpu.make_async_remote_copy(
            src_ref=buf.at[slot],
            dst_ref=buf.at[slot],
            send_sem=send_sem.at[which],
            recv_sem=recv_sem.at[which],
            device_id=peer,
            device_id_type=MESH,
        ).start()

    def arrived(sem, buf, which, count):
        part = buf.at[pl.ds(0, count)]
        pltpu.make_async_copy(part, part, sem.at[which]).wait()

    for step in hist_steps:
        send(a_buf, hist, 0, hist_peer(step))

    for copy in small_copies[2:]:
        copy.wait()

    row = lax.broadcasted_iota(jnp.int32, TILE, 0)
    lane = lax.broadcasted_iota(jnp.int32, TILE, 1)
    field = jnp.full((1, 128), t_sm[0, 0], jnp.int32).astype(jnp.float32) * FIELD_STEP
    momentum = ids_vm[...].reshape(1, 128)
    along_x = 2.0 * math.pi * (momentum & (LK - 1)).astype(jnp.float32) / LK
    along_y = 2.0 * math.pi * (momentum >> 6).astype(jnp.float32) / (total // LK)
    energy = -2.0 * (jnp.cos(along_x - field) + jnp.cos(along_y - field))
    angle = HOPPING_TIME * energy
    cosine = jnp.broadcast_to(jnp.cos(angle), TILE)
    sine = jnp.broadcast_to(jnp.sin(angle), TILE)
    before = jnp.concatenate(
        [prev_vm[r, a, c : c + 1, :] for c in range(2) for r in range(2) for a in range(2)], axis=0
    )
    is_real = (row & 2) == 0

    live_scale = jnp.where(live256, jnp.float32(1.0 / total), jnp.float32(0.0))
    real_side, imag_side = [], []
    for b in range(2):
        cr = coup_vm[0, b] * live_scale
        ci = coup_vm[1, b] * live_scale
        real_side.append(jnp.concatenate([cr, cr, -ci, -ci], axis=0))
        imag_side.append(jnp.concatenate([ci, ci, cr, cr], axis=0))

    upper = row >= 4
    live = jnp.where(upper, lane + 128, lane) < length
    drives = halves(src_vm[...])
    drive_scale = jnp.where(live, jnp.float32(TIME_STEP), jnp.float32(0.0))

    def bring(value, index):
        return pltpu.roll(value, 8 - index, axis=0) if index else value

    drive = [bring(drives, n) * drive_scale for n in range(4)]
    retain = []
    for n in range(4):
        decay = jnp.exp(-(jnp.full(TILE, rates_sm[n], jnp.float32) / slots))
        retain.append(jnp.where(live, decay, jnp.float32(1.0)))

    arrived(recv_sem, a_buf, 0, n_hist - 1)
    memory = a_buf[0]
    for h in range(1, n_hist):
        memory = memory + a_buf[h]
    summed = before + memory
    swapped = jnp.where(is_real, pltpu.roll(summed, 6, axis=0), -pltpu.roll(summed, 2, axis=0))
    current = cosine * summed + sine * swapped
    for c in range(2):
        for r in range(2):
            for a in range(2):
                at = 4 * c + 2 * r + a
                prop_out[r, a, c : c + 1, :] = current[at : at + 1, :]

    straight = jnp.concatenate([current[0:4], current[4:8]], axis=1)
    turned = jnp.concatenate([straight[2:4], -straight[0:2]], axis=0)
    rows = []
    for side in (straight, turned):
        twice = jnp.concatenate([side[i // 2 : i // 2 + 1] for i in range(8)], axis=0)
        rows.append(split_rows(twice).astype(jnp.bfloat16))
    contract_first = (((1,), (0,)), ((), ()))
    real_sum, imag_sum = None, None
    for b in range(2):
        out = jnp.zeros((16, 256), jnp.float32)
        for r in range(2):
            for part in (ghi, glo):
                out += lax.dot_general(
                    rows[r], part[r, b], contract_first, preferred_element_type=jnp.float32
                )
        both = out[0:8] + out[8:16]
        re, im = both * real_side[b], both * imag_side[b]
        real_sum = re if b == 0 else real_sum + re
        imag_sum = im if b == 0 else imag_sum + im

    def fold(value):
        first, second = value[:, :128], value[:, 128:]
        first = first + pltpu.roll(first, 4, axis=0)
        second = second + pltpu.roll(second, 4, axis=0)
        return jnp.where(upper, second, first)

    zr_buf[z] = fold(real_sum)
    pl.semaphore_wait(token_sem.at[0], 2)
    for step in z_steps:
        send(zr_buf, z, 1, z_peer(step))
    pi_buf[core] = fold(imag_sum)
    send(pi_buf, core, 4, partner)
    arrived(recv_sem, pi_buf, 4, 1)
    zi_buf[z] = pi_buf[0] + pi_buf[1]
    for step in z_steps:
        send(zi_buf, z, 2, z_peer(step))

    def total_over_z(buf, which):
        arrived(recv_sem, buf, which, n_z - 1)
        value = buf[0]
        for i in range(1, n_z):
            value = value + buf[i]
        return value

    pr_buf[core] = total_over_z(zr_buf, 1)
    send(pr_buf, core, 3, partner)
    arrived(recv_sem, pr_buf, 3, 1)
    delta_re = pr_buf[0] + pr_buf[1]

    d00, d01, d10, d11 = (TIME_STEP * bring(delta_re, i) for i in range(4))
    maps = (
        retain[0],
        retain[1] - d00,
        -d01,
        -d10,
        retain[2] - d11,
        retain[3] - (d00 + d11),
        *drive,
    )
    shift = 1
    while shift < 128:
        inside = lane >= shift
        early = tuple(
            jnp.where(inside, pltpu.roll(part, shift, axis=1), jnp.float32(one))
            for part, one in zip(maps, IDENTITY)
        )
        maps = compose(maps, early)
        shift *= 2
    ends = tuple(jnp.broadcast_to(part[:, 127:128], TILE) for part in maps)
    first_half = tuple(pltpu.roll(part, 4, axis=0) for part in ends)
    block = compose(ends, first_half)
    packed = jnp.zeros(TILE, jnp.float32)
    for i, part in enumerate(block):
        packed = jnp.where(lane == i, part, packed)
    c_buf[hist] = packed[4:5, :]
    for step in hist_steps:
        send(c_buf, hist, 5, hist_peer(step))

    prefix = compose(
        maps,
        tuple(
            jnp.where(upper, part, jnp.float32(one)) for part, one in zip(first_half, IDENTITY)
        ),
    )
    arrived(recv_sem, c_buf, 5, n_hist - 1)
    gathered = c_buf[...].reshape(n_hist, 128)
    for i in range(10):
        c_rows[i] = jnp.broadcast_to(gathered[:, i : i + 1], (n_hist, 128))
    state = tuple(jnp.full((1, 128), init_sm[n], jnp.float32) for n in range(4))
    start = state
    for j in range(n_hist):
        state = apply_map(tuple(c_rows[i, j : j + 1, :] for i in range(10)), state)
        if j + 1 < n_hist:
            mine = hist == j + 1
            start = tuple(jnp.where(mine, new, old) for new, old in zip(state, start))
    states = apply_map(prefix, tuple(jnp.broadcast_to(part, TILE) for part in start))
    for n in range(4):
        pp_out[n : n + 1, 0:128] = states[n][0:1]
        pp_out[n : n + 1, 128:256] = states[n][4:5]
    norm = state[0] * state[0] + state[1] * state[1] + state[2] * state[2] + state[3] * state[3]
    scale = jnp.broadcast_to(1.0 / jnp.sqrt(1.0 + norm), TILE)
    delta_im = total_over_z(zi_buf, 2)
    for r, delta in ((0, delta_re), (1, delta_im)):
        scaled = delta * scale
        for a in range(2):
            for half in range(2):
                hyb_out[r, a, :, half * 128 : half * 128 + 128] = scaled[
                    half * 4 + 2 * a : half * 4 + 2 * a + 2
                ]

    for buf, which, count in (
        (a_buf, 0, n_hist - 1),
        (zr_buf, 1, n_z - 1),
        (zi_buf, 2, n_z - 1),
        (pr_buf, 3, 1),
        (pi_buf, 4, 1),
        (c_buf, 5, n_hist - 1),
    ):
        arrived(send_sem, buf, which, count)


def put_out(*refs):
    sem = refs[6]
    copies = [pltpu.make_async_copy(refs[i], refs[3 + i], sem.at[i]) for i in range(3)]
    for copy in copies:
        copy.start()
    for copy in copies:
        copy.wait()


def on_device(sizes, *args):
    f32 = jnp.float32
    n_mom, n_hist = sizes
    n_z = n_mom // 2
    shapes = ((2, 2, 2, 128), (4, 256), (2, 2, 2, 256))
    hbm = pl.BlockSpec(memory_space=pltpu.HBM)
    vmem = pl.BlockSpec(memory_space=pltpu.VMEM)
    results = pl.pallas_call(
        functools.partial(kernel, sizes),
        out_shape=tuple(pltpu.VMEM(shape, f32) for shape in shapes),
        in_specs=[hbm] * 10,
        out_specs=(vmem, vmem, vmem),
        scratch_shapes=[
            pltpu.VMEM((2, 2, 2, 128, 256), f32),
            pltpu.VMEM((2, 2, 256, 256), jnp.bfloat16),
            pltpu.VMEM((2, 2, 256, 256), jnp.bfloat16),
            pltpu.VMEM((2, 2, 2, 256), f32),
            pltpu.VMEM((2, 2, 2, 256), f32),
            pltpu.VMEM((2, 2, 2, 128), f32),
            pltpu.VMEM((4, 256), f32),
            pltpu.VMEM((128,), jnp.int32),
            pltpu.SMEM((4,), f32),
            pltpu.SMEM((4,), f32),
            pltpu.SMEM((1, 1), jnp.int32),
            pltpu.SMEM((n_hist,), jnp.int32),
            pltpu.VMEM((n_hist, 8, 128), f32),
            pltpu.VMEM((n_z, 8, 128), f32),
            pltpu.VMEM((n_z, 8, 128), f32),
            pltpu.VMEM((2, 8, 128), f32),
            pltpu.VMEM((2, 8, 128), f32),
            pltpu.VMEM((n_hist, 1, 128), f32),
            pltpu.VMEM((10, n_hist, 128), f32),
            pltpu.SemaphoreType.DMA((13,)),
            pltpu.SemaphoreType.DMA((6,)),
            pltpu.SemaphoreType.DMA((6,)),
            pltpu.SemaphoreType.REGULAR((1,)),
        ],
        compiler_params=pltpu.CompilerParams(collective_id=0, has_side_effects=True),
        name="dmft_step",
    )(*args[:8], args[8].reshape(1, 1), args[9])
    return pl.pallas_call(
        put_out,
        out_shape=tuple(jax.ShapeDtypeStruct(shape, f32) for shape in shapes),
        in_specs=[vmem] * 3,
        out_specs=(hbm,) * 3,
        scratch_shapes=[pltpu.SemaphoreType.DMA((3,))],
        name="put_out",
    )(*(pltpu.with_memory_space_constraint(part, pltpu.VMEM) for part in results))


def solution(mesh):
    sizes = (mesh.shape["mom"], mesh.shape["hist"])
    placed = (
        P(None, None, None, "mom", "hist"),
        P(None, None, None, "hist"),
        P(None, None, None, "hist"),
        P(None, None, None, "mom"),
        P(),
        P(),
        P(None, "hist"),
        P("mom"),
        P(),
        P(),
    )
    return jax.shard_map(
        functools.partial(on_device, sizes),
        mesh=mesh,
        in_specs=placed,
        out_specs=(P(None, None, None, "mom"), P(None, "hist"), P(None, None, None, "hist")),
        check_vma=False,
    )
```
